256 devices in a mesh: seq: 64 (over z, y, core), slide: 4 (over x).
Axes of the slice: x: 4, y: 4, z: 8, core: 2. Of those that a mesh axis runs over, the one named last changes fastest.
Arguments:
- queries: bfloat16 [4, 8192, 768], P('slide', 'seq'), may hold values from -36 to 36
- keys: bfloat16 [4, 8192, 768], P('slide', 'seq'), may hold values from -6 to 6
- values: bfloat16 [4, 8192, 768], P('slide', 'seq'), may hold values from -6 to 6
- grad_out: bfloat16 [4, 8192, 768], P('slide', 'seq'), may hold values from -96 to 96
- w_out: bfloat16 [768, 768], replicated, may hold values from -0.21875 to 0.21875
- kept_tiles: int32 [4], P('slide'), may hold values from 2048 to 8192, as said below
Outputs:
- d_queries: bfloat16 [4, 8192, 768], P('slide', 'seq')
- d_keys: bfloat16 [4, 8192, 768], P('slide', 'seq')
- d_values: bfloat16 [4, 8192, 768], P('slide', 'seq')
- d_w_out: float32 [768, 768], replicated
The draws below stay inside these ranges and needn't reach their ends.
Inputs may be any that keep to these rules, and one draw needn't show every extreme that they name: `kept_tiles`: at least one slide keeps all 8192 positions.
All inputs are finite; a program needn't handle non-finite values.
Results may differ from the reference program's by a relative error of at most 0.023.
Values may be sent and summed in bfloat16 or wider, within the bound.
A program may use at most 64 MiB of HBM per device.

```python
import jax
import jax.numpy as jnp
from jax import lax

D = 768
HEADS = 16
DILATION_RATE = 16
SLIDES = 4
SEQ = 8192
SEG = 512
SELECTED_COUNT = 512


def draw_queries(key, part):
    drawn = jax.random.normal(jax.random.fold_in(key, 1), (SLIDES, SEQ, D), jnp.float32)
    return jnp.clip(drawn, -6.0, 6.0).astype(jnp.bfloat16)


def draw_keys(key, part):
    drawn = jax.random.normal(jax.random.fold_in(key, 2), (SLIDES, SEQ, D), jnp.float32)
    return jnp.clip(drawn, -6.0, 6.0).astype(jnp.bfloat16)


def draw_kept_tiles(key, part):
    counts = jax.random.randint(jax.random.fold_in(key, 5), (SLIDES,), SEQ // 4, SEQ + 1)
    chosen = jax.random.randint(jax.random.fold_in(key, 6), (), 0, SLIDES)
    return jnp.where(jnp.arange(SLIDES) == chosen, SEQ, counts).astype(jnp.int32)


def level_of(rng, extent, pieces, smallest, high):
    level = 1.0
    for position, shards_of in pieces:
        draws = jax.random.uniform(jax.random.fold_in(jax.random.fold_in(rng, 6), position), (shards_of,), jnp.float32, smallest / len(pieces), high / len(pieces))
        level = level * jnp.repeat(jnp.exp(draws), extent[position] // shards_of).reshape((-1,) + (1,) * (len(extent) - 1 - position))
    return level


def centred(own_key, extent, spread, reach, pieces=(), kind=jnp.bfloat16):
    loudness = level_of(own_key, extent, pieces, -0.22, 0.18) if pieces else 1.0
    array = jax.random.normal(own_key, extent, jnp.float32) * spread * loudness
    return jnp.minimum(jnp.maximum(array, -reach), reach).astype(kind)


def setup_inputs(seed: int = 0) -> dict:
    splits = jax.random.split(jax.random.key(seed), 7)
    return {
        "queries": draw_queries(jax.random.fold_in(splits[6], 71), 0),
        "keys": draw_keys(jax.random.fold_in(splits[6], 71), 0),
        "values": centred(splits[2], (SLIDES, SEQ, D), 1.0, 6.0, ((0, 4), (1, 64))),
        "grad_out": centred(splits[3], (SLIDES, SEQ, D), 16.0, 96.0, ((0, 4), (1, 64))),
        "w_out": centred(splits[4], (D, D), D ** -0.5, 0.21875),
        "kept_tiles": draw_kept_tiles(jax.random.fold_in(splits[6], 71), 0),
    }


def head_pass(query_rows, key_rows, value_rows, grad_rows, key_valid, row_valid, scaling):
    query_f = query_rows.astype(jnp.float32)
    key_f = key_rows.astype(jnp.float32)
    value_f = value_rows.astype(jnp.float32)
    grad_f = grad_rows.astype(jnp.float32)
    scores = jnp.einsum("qhd,khd->hqk", query_f, key_f) * scaling
    scores = jnp.where(key_valid[:, None, :], scores, -1e30)
    row_max = jnp.max(scores, axis=-1, keepdims=True)
    log_norm = row_max + jnp.log(jnp.sum(jnp.exp(scores - row_max), axis=-1, keepdims=True))
    probs = jnp.exp(scores - log_norm)
    probs_low = probs.astype(jnp.bfloat16)
    mixed = jnp.einsum("hqk,khd->qhd", probs_low.astype(jnp.float32), value_f)
    attn_low = (mixed * row_valid[:, :, None]).astype(jnp.bfloat16)
    d_probs = jnp.einsum("qhd,khd->hqk", grad_f, value_f)
    row_dot = jnp.transpose(jnp.sum(grad_f * attn_low.astype(jnp.float32), axis=-1))[:, :, None]
    d_scores = (probs * (d_probs - row_dot)).astype(jnp.bfloat16)
    scores_f = d_scores.astype(jnp.float32)
    d_query = jnp.einsum("hqk,khd->qhd", scores_f, key_f) * scaling
    d_key = jnp.einsum("hqk,qhd->khd", scores_f, query_f) * scaling
    d_value = jnp.einsum("hqk,qhd->khd", probs_low.astype(jnp.float32), grad_f)
    return attn_low, d_query, d_key, d_value


def dilated_rows(tile_block, heads_of_group):
    group_layout = tile_block.reshape(tile_block.shape[0] // DILATION_RATE, DILATION_RATE, heads_of_group, -1)
    return jnp.stack([group_layout[:, head, head] for head in range(heads_of_group)], axis=1)


def spread_rows(selected_rows, heads_of_group):
    indicator_matrix = (jnp.arange(DILATION_RATE)[:, None] == jnp.arange(heads_of_group)[None, :]).astype(selected_rows.dtype)
    complete_rows = selected_rows[:, None, :, :] * indicator_matrix[None, :, :, None]
    return complete_rows.reshape(selected_rows.shape[0] * DILATION_RATE, -1)


def reference(queries, keys, values, grad_out, w_out, kept_tiles):
    head_dim = D // HEADS
    half_width = D // 2
    heads_of_group = HEADS // 2
    scaling = head_dim ** -0.5
    segments = SEQ // SEG
    weight_sum = jnp.zeros((D, D), jnp.float32)
    grads_q, grads_k, grads_v = [], [], []
    for slide_num in range(SLIDES):
        token_positions = jnp.arange(SEQ)
        kept_count = kept_tiles[slide_num]
        key_ok = token_positions < kept_count
        row_valid = key_ok.astype(jnp.float32)
        grad_rows = grad_out[slide_num]
        d_attn = (jnp.dot(grad_rows, w_out.T, preferred_element_type=jnp.float32) * row_valid[:, None]).astype(jnp.bfloat16)

        def shape_near(tile_block):
            return tile_block[:, :half_width].reshape(segments, SEG, heads_of_group, head_dim)

        def segment_pass(items):
            query_seg, key_seg, value_seg, grad_seg, valid_seg, rows_seg = items
            return head_pass(query_seg, key_seg, value_seg, grad_seg, valid_seg[None, :], rows_seg[:, None], scaling)

        attn_near, dq_near, dk_near, dv_near = lax.map(segment_pass, (
            shape_near(queries[slide_num]), shape_near(keys[slide_num]), shape_near(values[slide_num]),
            shape_near(d_attn), key_ok.reshape(segments, SEG), row_valid.reshape(segments, SEG)))
        attn_near = attn_near.reshape(SEQ, half_width)
        dq_near = dq_near.reshape(SEQ, half_width)
        dk_near = dk_near.reshape(SEQ, half_width)
        dv_near = dv_near.reshape(SEQ, half_width)

        far_q = dilated_rows(queries[slide_num][:, half_width:], heads_of_group)
        far_k = dilated_rows(keys[slide_num][:, half_width:], heads_of_group)
        far_v = dilated_rows(values[slide_num][:, half_width:], heads_of_group)
        far_g = dilated_rows(d_attn[:, half_width:], heads_of_group)
        selected_positions = jnp.arange(SELECTED_COUNT)[:, None] * DILATION_RATE + jnp.arange(heads_of_group)[None, :]
        sel_valid = selected_positions < kept_count
        attn_far, dq_far, dk_far, dv_far = head_pass(far_q, far_k, far_v, far_g, sel_valid.T, sel_valid.astype(jnp.float32), scaling)

        attn = jnp.concatenate([attn_near, spread_rows(attn_far, heads_of_group)], axis=1)
        weight_sum = weight_sum + jnp.dot(attn.T, grad_rows, preferred_element_type=jnp.float32)
        grads_q.append(jnp.concatenate([dq_near, spread_rows(dq_far, heads_of_group)], axis=1).astype(jnp.bfloat16))
        grads_k.append(jnp.concatenate([dk_near, spread_rows(dk_far, heads_of_group)], axis=1).astype(jnp.bfloat16))
        grads_v.append(jnp.concatenate([dv_near, spread_rows(dv_far, heads_of_group)], axis=1).astype(jnp.bfloat16))
    d_w_out = weight_sum * (SLIDES * SEQ) ** -0.5
    return jnp.stack(grads_q), jnp.stack(grads_k), jnp.stack(grads_v), d_w_out
```

```python
import jax
import jax.numpy as jnp
from jax import lax
from jax.experimental import pallas as pl
from jax.experimental.pallas import tpu as pltpu
from jax.sharding import PartitionSpec as P

ROWS = 128
WIDTH = 768
HALF = 384
HD = 48
SEG = 512
F32 = jnp.float32
BF16 = jnp.bfloat16
MESH = pl.DeviceIdType.MESH
NN = (((1,), (0,)), ((), ()))
NT = (((1,), (1,)), ((), ()))


def dot(a, b, dims=NN):
    return lax.dot_general(a, b, dims, preferred_element_type=F32)


def iota(shape, dim):
    return lax.broadcasted_iota(jnp.int32, shape, dim)


def one_hot(mask):
    return jnp.where(mask, 1.0, 0.0).astype(BF16)


def turn(a):
    return jnp.transpose(a.astype(F32)).astype(BF16)


def head_pass(q_t, k_t, v_t, o_t, key_ok, row_ok):
    scaling = HD ** -0.5
    scores = dot(turn(k_t), q_t) * scaling
    scores = jnp.where(key_ok, scores, -1e30)
    top = jnp.max(scores, axis=0, keepdims=True)
    grown = jnp.exp(scores - top)
    probs = grown * (1.0 / jnp.sum(grown, axis=0, keepdims=True))
    low = probs.astype(BF16)
    attn = (dot(v_t, low) * row_ok).astype(BF16)
    d_probs = dot(turn(v_t), o_t)
    row_dot = jnp.sum(o_t.astype(F32) * attn.astype(F32), axis=0, keepdims=True)
    d_scores = (probs * (d_probs - row_dot)).astype(BF16)
    d_q = (dot(k_t, d_scores) * scaling).astype(BF16)
    d_k = (dot(q_t, d_scores, NT) * scaling).astype(BF16)
    d_v = dot(o_t, low, NT).astype(BF16)
    return attn, d_q, d_k, d_v


def owner_of(j):
    return 8 * j + 2 * (j % 4) + j // 4


def kernel(
    kept_ref, q_ref, k_ref, v_ref, g_ref, w_ref,
    dq_ref, dk_ref, dv_ref, dw_ref,
    a_send, a_recv, a_back, a_ret, b_send, b_recv, b_back, b_ret,
    part, c_send, c_recv, h_ref, s1_send, s1_recv, s2_own, s2_send, s2_recv,
    z_buf, g1, g2, g3,
    a_ss, a_rs, ar_ss, ar_rs, b_ss, b_rs, br_ss, br_rs, c_ss, c_rs,
    s1_ss, s1_rs, s2_ss, s2_rs, z_ss, z_rs, g1_ss, g1_rs, g2_ss, g2_rs, g3_ss, g3_rs,
):
    seq = lax.axis_index("seq")
    x = lax.axis_index("slide")
    core = seq % 2
    y = (seq // 2) % 4
    z = seq // 8
    pos = seq % 4
    first = seq - pos
    is_owner = seq == owner_of(z)

    def x_peer(r):
        return (seq, (x + r) % 4)

    def y_peer(r):
        return ((z * 4 + (y + r) % 4) * 2 + core, x)

    def z_peer(r):
        return ((((z + r) % 8) * 4 + y) * 2 + core, x)

    partner = (seq + 1 - 2 * core, x)

    def send(src, dst, ss, rs, device):
        copy = pltpu.make_async_remote_copy(
            src_ref=src, dst_ref=dst, send_sem=ss, recv_sem=rs,
            device_id=device, device_id_type=MESH,
        )
        copy.start()
        return copy

    barrier = pltpu.get_barrier_semaphore()

    def greet(device):
        pl.semaphore_signal(barrier, inc=1, device_id=device, device_id_type=MESH)

    greet(partner)
    for r in range(1, 4):
        greet((first + (pos + r) % 4, x))
        greet(x_peer(r))
        greet(y_peer(r))
    for r in range(1, 8):
        greet(z_peer(r))

    def greet_owner(j, carry):
        @pl.when(owner_of(j) != seq)
        def _():
            greet((owner_of(j), x))
        return carry

    lax.fori_loop(0, 8, greet_owner, 0)

    @pl.when(is_owner)
    def _():
        def greet_all(r, carry):
            greet(((seq + r) % 64, x))
            return carry
        lax.fori_loop(1, 64, greet_all, 0)

    kept = kept_ref[0]
    half = pl.ds(HALF, HALF)

    col_ok = jnp.where(seq * ROWS + iota((1, ROWS), 1) < kept, 1.0, 0.0)
    grad = g_ref[...]
    d_attn = (dot(w_ref[...], grad, NT) * col_ok).astype(BF16)
    near = (turn(q_ref[:, :HALF]), turn(k_ref[:, :HALF]), turn(v_ref[:, :HALF]), d_attn[:HALF])
    for d in range(4):
        for t in range(4):
            a_send[d, 96 * t : 96 * t + 96, :] = near[t][96 * d : 96 * d + 96]
    a_recv[pos] = a_send[pos]

    r64 = iota((64, ROWS), 0)
    pick = one_hot(iota((64, ROWS), 1) == 16 * (r64 & 7) + (r64 >> 3))
    l_in = iota((64, HALF), 1) - HD * (iota((64, HALF), 0) >> 3)
    own_lanes = (l_in >= 0) & (l_in < HD)
    feat = iota((HALF, ROWS), 0)
    feat = feat - HD * ((feat * 683) >> 15)
    lane = iota((HALF, ROWS), 1)
    fold0 = one_hot(lane == feat)
    fold1 = one_hot(lane == feat + HD)

    def far(block, dims=NN):
        rows = dot(pick, block, dims)
        return jnp.where(own_lanes, rows, 0.0).astype(BF16)

    far_qk = dot(far(q_ref[:, half]), fold0) + dot(far(k_ref[:, half]), fold1)
    far_vo = dot(far(v_ref[:, half]), fold0) + dot(far(d_attn[HALF:], NT), fold1)
    b_send[...] = jnp.concatenate(
        [far_qk.reshape(8, 8, ROWS), far_vo.reshape(8, 8, ROWS)], axis=1
    ).astype(BF16)

    pl.semaphore_wait(barrier, 17 + jnp.where(is_owner, 70, 8))

    def b_copy(j):
        return pltpu.make_async_remote_copy(
            src_ref=b_send.at[j], dst_ref=b_recv.at[seq], send_sem=b_ss.at[j], recv_sem=b_rs,
            device_id=(owner_of(j), x), device_id_type=MESH,
        )

    def b_start(j, carry):
        @pl.when(owner_of(j) != seq)
        def _():
            b_copy(j).start()
        return carry

    lax.fori_loop(0, 8, b_start, 0)

    @pl.when(is_owner)
    def _():
        pltpu.make_async_copy(b_send.at[z], b_recv.at[seq], b_rs).start()

    a_copies = []
    for r in range(1, 4):
        d = (pos + r) % 4
        a_copies.append(
            send(a_send.at[d], a_recv.at[pos], a_ss.at[r - 1], a_rs.at[r - 1], (first + d, x))
        )
    for copy in a_copies:
        copy.wait_recv()

    at = first * ROWS
    key_ok = at + iota((SEG, 1), 0) < kept
    row_ok = jnp.where(at + iota((1, SEG), 1) < kept, 1.0, 0.0)
    for h in range(2):
        parts = [
            jnp.concatenate(
                [a_recv[s, 96 * t + HD * h : 96 * t + HD * h + HD, :] for s in range(4)], axis=1
            )
            for t in range(4)
        ]
        outs = head_pass(*parts, key_ok, row_ok)
        for t in range(4):
            for d in range(4):
                a_back[d, 96 * t + HD * h : 96 * t + HD * h + HD, :] = outs[t][
                    :, ROWS * d : ROWS * d + ROWS
                ]
    a_ret[pos] = a_back[pos]
    for r in range(1, 4):
        d = (pos + r) % 4
        a_copies.append(
            send(a_back.at[d], a_ret.at[pos], ar_ss.at[r - 1], ar_rs.at[r - 1], (first + d, x))
        )

    def back_copy(s):
        return pltpu.make_async_remote_copy(
            src_ref=b_back.at[s], dst_ref=b_ret.at[z], send_sem=br_ss, recv_sem=br_rs,
            device_id=(s, x), device_id_type=MESH,
        )

    @pl.when(is_owner)
    def _():
        pltpu.make_async_copy(b_recv, b_recv, b_rs).wait()
        rows = b_recv[...].astype(F32)
        qk = turn(rows[:, :8, :].reshape(SEG, ROWS))
        vo = turn(rows[:, 8:, :].reshape(SEG, ROWS))
        key_ok = 16 * iota((SEG, 1), 0) + z < kept
        row_ok = jnp.where(16 * iota((1, SEG), 1) + z < kept, 1.0, 0.0)
        outs = head_pass(
            qk[:HD], qk[HD : 2 * HD], vo[:HD], vo[HD : 2 * HD], key_ok, row_ok
        )
        pad = jnp.zeros((ROWS - 2 * HD, SEG), F32)
        packs = [
            jnp.transpose(
                jnp.concatenate([outs[t].astype(F32), outs[t + 1].astype(F32), pad], axis=0)
            ).reshape(64, 8, ROWS)
            for t in (0, 2)
        ]
        b_back[...] = jnp.concatenate(packs, axis=1).astype(BF16)

        def back(r, carry):
            back_copy((seq + r) % 64).start()
            return carry

        lax.fori_loop(1, 64, back, 0)
        pltpu.make_async_copy(b_back.at[seq], b_ret.at[z], br_rs).start()

    for copy in a_copies[3:]:
        copy.wait_recv()
    near_out = [
        jnp.concatenate([a_ret[s, 96 * t : 96 * t + 96, :] for s in range(4)], axis=0)
        for t in range(4)
    ]
    part[:HALF, :] = dot(near_out[0], grad)
    for t, ref in ((1, dq_ref), (2, dk_ref), (3, dv_ref)):
        ref[:, :HALF] = turn(near_out[t])

    pltpu.make_async_copy(b_ret, b_ret, br_rs).wait()
    rows = b_ret[...].astype(F32)
    back_ad = rows[:, :8, :].reshape(64, ROWS).astype(BF16)
    back_kv = rows[:, 8:, :].reshape(64, ROWS).astype(BF16)
    t_in = iota((HALF, 64), 0) - HD * (iota((HALF, 64), 1) >> 3)
    own_rows = (t_in >= 0) & (t_in < HD)
    r64 = iota((ROWS, 64), 1)
    place = one_hot(iota((ROWS, 64), 0) == 16 * (r64 & 7) + (r64 >> 3))
    attn_far = jnp.where(own_rows, dot(fold0, back_ad, NT), 0.0).astype(BF16)
    part[HALF:, :] = dot(attn_far, dot(pick, grad).astype(BF16))

    def spread(block, fold):
        rows = jnp.where(own_lanes, dot(block, fold, NT), 0.0).astype(BF16)
        return dot(place, rows).astype(BF16)

    dq_ref[:, half] = spread(back_ad, fold1)
    dk_ref[:, half] = spread(back_kv, fold0)
    dv_ref[:, half] = spread(back_kv, fold1)

    there = pl.multiple_of((1 - core) * HALF, HALF)
    here = pl.multiple_of(core * HALF, HALF)
    c_send[...] = part[pl.ds(there, HALF), :].astype(BF16)
    c_copy = send(c_send, c_recv, c_ss, c_rs, partner)
    c_copy.wait_recv()
    total = part[pl.ds(here, HALF), :] + c_recv[...].astype(F32)
    for i in range(2):
        block = total[:, HALF * i : HALF * i + HALF].reshape(4, 96, HALF)
        h_ref[i] = block
        s1_send[i] = block.astype(BF16)
    own = (x, y)
    peers = (x_peer, y_peer)

    copies = [c_copy]
    step = []
    for r in range(1, 4):
        for i in range(2):
            step.append(
                send(
                    s1_send.at[i, (own[i] + r) % 4], s1_recv.at[i, r - 1],
                    s1_ss.at[i, r - 1], s1_rs.at[i, r - 1], peers[i](r),
                )
            )
    for copy in step:
        copy.wait_recv()
    copies += step
    for i in range(2):
        block = h_ref[i, own[i]]
        for r in range(3):
            block += s1_recv[i, r].astype(F32)
        block = block.reshape(4, 24, HALF)
        s2_own[i] = block
        s2_send[i] = block.astype(BF16)
    step = []
    for r in range(1, 4):
        for i in range(2):
            step.append(
                send(
                    s2_send.at[i, (own[1 - i] + r) % 4], s2_recv.at[i, r - 1],
                    s2_ss.at[i, r - 1], s2_rs.at[i, r - 1], peers[1 - i](r),
                )
            )
    for copy in step:
        copy.wait_recv()
    copies += step
    for i in range(2):
        block = s2_own[i, own[1 - i]]
        for r in range(3):
            block += s2_recv[i, r].astype(F32)
        z_buf[z, i] = block.astype(BF16)
    step = []
    for r in range(1, 8):
        step.append(send(z_buf.at[z], z_buf.at[z], z_ss.at[r - 1], z_rs.at[r - 1], z_peer(r)))
    for copy in step:
        copy.wait_recv()
    copies += step
    scale = (32768.0) ** -0.5
    for i in range(2):
        block = z_buf[0, i].astype(F32)
        for r in range(1, 8):
            block += z_buf[r, i].astype(F32)
        g1[i, own[1 - i]] = (block * scale).astype(BF16)
    step = []
    for r in range(1, 4):
        for i in range(2):
            piece = g1.at[i, own[1 - i]]
            step.append(
                send(piece, piece, g1_ss.at[i, r - 1], g1_rs.at[i, r - 1], peers[1 - i](r))
            )
    for copy in step:
        copy.wait_recv()
    copies += step
    for i in range(2):
        g2[i, own[i]] = g1[i]
    step = []
    for r in range(1, 4):
        for i in range(2):
            step.append(
                send(
                    g1.at[i], g2.at[i, own[i]],
                    g2_ss.at[i, r - 1], g2_rs.at[i, r - 1], peers[i](r),
                )
            )
    for copy in step:
        copy.wait_recv()
    copies += step
    last = send(g2, g3, g3_ss, g3_rs, partner)
    copies.append(last)
    for i in range(2):
        dw_ref[pl.ds(here, HALF), HALF * i : HALF * i + HALF] = (
            g2[i].astype(F32).reshape(HALF, HALF)
        )
    last.wait_recv()
    for i in range(2):
        dw_ref[pl.ds(there, HALF), HALF * i : HALF * i + HALF] = (
            g3[i].astype(F32).reshape(HALF, HALF)
        )

    for copy in a_copies + copies:
        copy.wait_send()

    def b_done(j, carry):
        @pl.when(owner_of(j) != seq)
        def _():
            b_copy(j).wait_send()
        return carry

    lax.fori_loop(0, 8, b_done, 0)

    @pl.when(is_owner)
    def _():
        part_of = b_back.at[pl.ds(0, 63)]
        pltpu.make_async_remote_copy(
            src_ref=part_of, dst_ref=part_of, send_sem=br_ss, recv_sem=br_rs,
            device_id=partner, device_id_type=MESH,
        ).wait_send()


def per_device(queries, keys, values, grad_out, w_out, kept_tiles):
    vmem = pl.BlockSpec(memory_space=pltpu.VMEM)
    dma = pltpu.SemaphoreType.DMA
    block = jax.ShapeDtypeStruct((ROWS, WIDTH), BF16)
    outs = pl.pallas_call(
        kernel,
        out_shape=(block, block, block, jax.ShapeDtypeStruct((WIDTH, WIDTH), F32)),
        in_specs=[pl.BlockSpec(memory_space=pltpu.SMEM)] + [vmem] * 5,
        out_specs=(vmem,) * 4,
        scratch_shapes=[
            pltpu.VMEM((4, HALF, ROWS), BF16),
            pltpu.VMEM((4, HALF, ROWS), BF16),
            pltpu.VMEM((4, HALF, ROWS), BF16),
            pltpu.VMEM((4, HALF, ROWS), BF16),
            pltpu.VMEM((8, 16, ROWS), BF16),
            pltpu.VMEM((64, 16, ROWS), BF16),
            pltpu.VMEM((64, 16, ROWS), BF16),
            pltpu.VMEM((8, 16, ROWS), BF16),
            pltpu.VMEM((WIDTH, WIDTH), F32),
            pltpu.VMEM((HALF, WIDTH), BF16),
            pltpu.VMEM((HALF, WIDTH), BF16),
            pltpu.VMEM((2, 4, 96, HALF), F32),
            pltpu.VMEM((2, 4, 96, HALF), BF16),
            pltpu.VMEM((2, 3, 96, HALF), BF16),
            pltpu.VMEM((2, 4, 24, HALF), F32),
            pltpu.VMEM((2, 4, 24, HALF), BF16),
            pltpu.VMEM((2, 3, 24, HALF), BF16),
            pltpu.VMEM((8, 2, 24, HALF), BF16),
            pltpu.VMEM((2, 4, 24, HALF), BF16),
            pltpu.VMEM((2, 4, 4, 24, HALF), BF16),
            pltpu.VMEM((2, 4, 4, 24, HALF), BF16),
            dma((3,)), dma((3,)), dma((3,)), dma((3,)),
            dma((8,)), dma, dma, dma, dma, dma,
            dma((2, 3)), dma((2, 3)), dma((2, 3)), dma((2, 3)), dma((7,)), dma((7,)),
            dma((2, 3)), dma((2, 3)), dma((2, 3)), dma((2, 3)), dma, dma,
        ],
        compiler_params=pltpu.CompilerParams(
            collective_id=0, has_side_effects=True, vmem_limit_bytes=56 * 1024 * 1024
        ),
        name="grouped_attention_grads",
    )(kept_tiles, queries[0], keys[0], values[0], grad_out[0], w_out)
    return (outs[0][None], outs[1][None], outs[2][None], outs[3])


def solution(mesh):
    rows = P("slide", "seq", None)
    return jax.shard_map(
        per_device,
        mesh=mesh,
        in_specs=(rows, rows, rows, rows, P(), P("slide")),
        out_specs=(rows, rows, rows, P()),
        check_vma=False,
    )
```

```python
import jax
import jax.numpy as jnp
from jax import lax
from jax.experimental import pallas as pl
from jax.experimental.pallas import tpu as pltpu
from jax.sharding import PartitionSpec as P

ROWS = 128
WIDTH = 768
HALF = 384
HD = 48
SEG = 512
PART = (24, HALF)
F32 = jnp.float32
BF16 = jnp.bfloat16
MESH = pl.DeviceIdType.MESH
NN = (((1,), (0,)), ((), ()))
NT = (((1,), (1,)), ((), ()))
SCALING = HD ** -0.5


def dot(a, b, dims=NN):
    return lax.dot_general(a, b, dims, preferred_element_type=F32)


def iota(shape, dim):
    return lax.broadcasted_iota(jnp.int32, shape, dim)


def one_hot(mask):
    return jnp.where(mask, 1.0, 0.0).astype(BF16)


def turn(a):
    return jnp.transpose(a.astype(F32)).astype(BF16)


def softmax(scores, key_ok):
    scores = jnp.where(key_ok, scores * SCALING, -1e30)
    grown = jnp.exp(scores - jnp.max(scores, axis=0, keepdims=True))
    return grown * (1.0 / jnp.sum(grown, axis=0, keepdims=True))


def kernel(
    kept_ref, q_ref, k_ref, v_ref, g_ref, w_ref,
    dq_ref, dk_ref, dv_ref, dw_ref,
    a_send, a_recv, a_back, a_ret, g_all, probs_ref, low_ref,
    b_send, b_recv, kv_all, dkv_send, dkv_recv, b_back, b_ret,
    pa_own, pa_send, pa_recv, pb_own, pb_send, pb_recv, za, tb, g1, g2, g3,
    a_ss, a_rs, ar_ss, ar_rs, gr_ss, gr_rs, b_ss, b_rs, kv_ss, kv_rs, dkv_ss, dkv_rs,
    br_ss, br_rs, pa_ss, pa_rs, pb_ss, pb_rs, za_ss, za_rs, tb_ss, tb_rs,
    g1a_ss, g1a_rs, g1b_ss, g1b_rs, g2_ss, g2_rs, g3_ss, g3_rs,
):
    seq = lax.axis_index("seq")
    x = lax.axis_index("slide")
    core = seq % 2
    y = (seq // 2) % 4
    z = seq // 8
    pos = seq % 4
    tee = seq % 8
    first = seq - pos
    m = y // 2

    def x_peer(r):
        return (seq, (x + r) % 4)

    def y_peer(r):
        return ((z * 4 + (y + r) % 4) * 2 + core, x)

    def z_peer(r):
        return (((z + r) % 8) * 8 + tee, x)

    def plane_peer(r):
        return (z * 8 + (tee + r) % 8, x)

    def xm_peer(rx, rm):
        return ((z * 4 + (y + 2 * rm) % 4) * 2 + core, (x + rx) % 4)

    partner = (seq + 1 - 2 * core, x)
    across = (first + (pos + 2) % 4, x)

    started = []

    def send(src, dst, ss, rs, device):
        copy = pltpu.make_async_remote_copy(
            src_ref=src, dst_ref=dst, send_sem=ss, recv_sem=rs,
            device_id=device, device_id_type=MESH,
        )
        copy.start()
        started.append(copy)
        return copy

    def arrived(copies):
        for copy in copies:
            copy.wait_recv()

    barrier = pltpu.get_barrier_semaphore()

    def greet(device):
        pl.semaphore_signal(barrier, inc=1, device_id=device, device_id_type=MESH)

    for r in range(1, 8):
        greet(z_peer(r))
    for r in range(1, 8):
        greet(plane_peer(r))
    for rx in range(1, 4):
        for rm in range(2):
            greet(xm_peer(rx, rm))

    kept = kept_ref[0]
    far = pl.ds(HALF, HALF)
    col_ok = jnp.where(seq * ROWS + iota((1, ROWS), 1) < kept, 1.0, 0.0)
    grad = g_ref[...]
    d_attn = (dot(w_ref[...], grad, NT) * col_ok).astype(BF16)
    near = (turn(q_ref[:, :HALF]), turn(k_ref[:, :HALF]), turn(v_ref[:, :HALF]), d_attn[:HALF])
    for d in range(4):
        for t in range(4):
            a_send[d, 96 * t : 96 * t + 96, :] = near[t][96 * d : 96 * d + 96]
    a_recv[pos] = a_send[pos]
    g_all[pos] = grad

    r64 = iota((64, ROWS), 0)
    pick = one_hot(iota((64, ROWS), 1) == 16 * (r64 & 7) + (r64 >> 3))
    l_in = iota((64, HALF), 1) - HD * (iota((64, HALF), 0) >> 3)
    own_lanes = (l_in >= 0) & (l_in < HD)
    feat = iota((HALF, ROWS), 0)
    feat = feat - HD * ((feat * 683) >> 15)
    lane = iota((HALF, ROWS), 1)
    fold0 = one_hot(lane == feat)
    fold1 = one_hot(lane == feat + HD)

    def dilated(block, dims=NN):
        rows = dot(pick, block, dims)
        return jnp.where(own_lanes, rows, 0.0).astype(BF16)

    def tops(block):
        return block.reshape(8, 8, block.shape[-1])

    far_ko = dot(dilated(k_ref[:, far]), fold0) + dot(dilated(d_attn[HALF:], NT), fold1)
    far_qv = dot(dilated(q_ref[:, far]), fold0) + dot(dilated(v_ref[:, far]), fold1)
    far_g = dot(pick, grad)
    b_send[:, :, :ROWS] = jnp.concatenate([tops(far_ko), tops(far_qv)], axis=1).astype(BF16)
    b_send[:, :, ROWS:] = jnp.concatenate(
        [tops(far_g[:, :HALF]), tops(far_g[:, HALF:])], axis=1
    ).astype(BF16)
    b_recv[z] = b_send[z]

    pl.semaphore_wait(barrier, 20)

    b_in = [
        send(b_send.at[(z + r) % 8], b_recv.at[z], b_ss.at[r - 1], b_rs.at[r - 1], z_peer(r))
        for r in (4, 3, 5, 2, 6, 1, 7)
    ]
    a_in = [
        send(
            a_send.at[(pos + r) % 4], a_recv.at[pos],
            a_ss.at[r - 1], a_rs.at[r - 1], (first + (pos + r) % 4, x),
        )
        for r in range(1, 4)
    ]
    g_across = send(g_ref, g_all.at[pos], gr_ss.at[0], gr_rs.at[0], across)
    g_near = send(g_ref, g_all.at[pos], gr_ss.at[1], gr_rs.at[1], partner)

    arrived(b_in)
    rows = b_recv[:, :, :ROWS].astype(F32)
    ko = rows[:, :8, :].reshape(64, ROWS)
    qv = rows[:, 8:, :].reshape(64, ROWS)
    lane64 = iota((64, ROWS), 1)
    left = lane64 < HD
    right = (lane64 >= HD) & (lane64 < 2 * HD)
    kv_all[tee] = jnp.where(left, ko, jnp.where(right, qv, 0.0)).astype(BF16)
    kv_in = [
        send(kv_all.at[tee], kv_all.at[tee], kv_ss.at[r - 1], kv_rs.at[r - 1], plane_peer(r))
        for r in range(1, 8)
    ]
    q_rows = jnp.where(left, qv, 0.0).astype(BF16)
    o_rows = jnp.where(right, ko, 0.0).astype(BF16)
    q_cols = turn(q_rows)
    o_cols = turn(o_rows)

    arrived(a_in)
    at = first * ROWS
    key_ok = at + iota((SEG, 1), 0) < kept
    row_ok = jnp.where(at + iota((1, SEG), 1) < kept, 1.0, 0.0)

    def head_rows(t, h):
        lo = 96 * t + HD * h
        return jnp.concatenate([a_recv[s, lo : lo + HD, :] for s in range(4)], axis=1)

    attn_near = []
    for h in range(2):
        probs = softmax(dot(turn(head_rows(1, h)), head_rows(0, h)), key_ok)
        low = probs.astype(BF16)
        probs_ref[h] = probs
        low_ref[h] = low
        attn_near.append((dot(head_rows(2, h), low) * row_ok).astype(BF16))

    arrived([g_across])
    g_fwd = send(
        g_all.at[(pos + 2) % 4], g_all.at[(pos + 2) % 4], gr_ss.at[2], gr_rs.at[2], partner
    )

    arrived(kv_in)
    kv = kv_all[...].reshape(SEG, ROWS)
    kv_cols = turn(kv)
    r512 = iota((SEG, 1), 0)
    far_key_ok = (
        (((r512 >> 3) & 7) * 8 + (r512 >> 6)) * ROWS + 16 * (r512 & 7) + z < kept
    )
    c64 = iota((1, 64), 1)
    far_row_ok = jnp.where(((c64 >> 3) * 8 + tee) * ROWS + 16 * (c64 & 7) + z < kept, 1.0, 0.0)
    far_probs = softmax(dot(kv, q_cols), far_key_ok)
    far_low = far_probs.astype(BF16)
    attn_far = (dot(kv_cols, far_low) * far_row_ok).astype(BF16)
    g_rows = b_recv[:, :, ROWS:].astype(F32)
    for i in range(2):
        block = dot(
            attn_far[HD : 2 * HD], g_rows[:, 8 * i : 8 * i + 8, :].reshape(64, HALF).astype(BF16)
        )
        for half in range(2):
            piece = block[24 * half : 24 * half + 24]
            pb_own[2 * half + i] = piece
            pb_send[2 * half + i] = piece.astype(BF16)
    pb_in = [
        send(pb_send.at[(x + r) % 4], pb_recv.at[r - 1], pb_ss.at[r - 1], pb_rs.at[r - 1], x_peer(r))
        for r in range(1, 4)
    ]

    arrived([g_near, g_fwd])
    attn = jnp.concatenate(attn_near, axis=0)
    block = dot(attn, g_all[...].reshape(SEG, WIDTH))
    for i in range(4):
        for j in range(2):
            piece = block[24 * i : 24 * i + 24, HALF * j : HALF * j + HALF]
            pa_own[i, j] = piece
            pa_send[i, j] = piece.astype(BF16)
    pa_in = [
        send(
            pa_send.at[(x + rx) % 4, (m + rm) % 2], pa_recv.at[2 * rx + rm - 1],
            pa_ss.at[2 * rx + rm - 1], pa_rs.at[2 * rx + rm - 1], xm_peer(rx, rm),
        )
        for rx, rm in ((2, 1), (1, 1), (3, 1), (2, 0), (1, 0), (3, 0), (0, 1))
    ]

    row_dot = jnp.sum(o_cols.astype(F32) * attn_far.astype(F32), axis=0, keepdims=True)
    far_ds = (far_probs * (dot(kv, o_cols) - row_dot)).astype(BF16)
    far_dq = jnp.transpose(dot(kv_cols, far_ds) * SCALING)
    dkv = dot(far_ds, q_rows) * SCALING + dot(far_low, o_rows)
    dkv = dkv.reshape(8, 64, ROWS)
    dkv_send[...] = dkv.astype(BF16)
    dkv_recv[tee] = dkv_send[tee]
    dkv_in = [
        send(
            dkv_send.at[(tee + r) % 8], dkv_recv.at[tee],
            dkv_ss.at[r - 1], dkv_rs.at[r - 1], plane_peer(r),
        )
        for r in range(1, 8)
    ]

    arrived(pb_in)
    piece = pb_own[x]
    for r in range(3):
        piece += pb_recv[r].astype(F32)
    tb[tee] = piece.astype(BF16)
    tb_in = [
        send(tb.at[tee], tb.at[tee], tb_ss.at[r - 1], tb_rs.at[r - 1], plane_peer(r))
        for r in range(1, 8)
    ]

    def near_back(h):
        q_t, k_t, v_t, o_t = (head_rows(t, h) for t in range(4))
        row_dot = jnp.sum(o_t.astype(F32) * attn_near[h].astype(F32), axis=0, keepdims=True)
        d_scores = (probs_ref[h] * (dot(turn(v_t), o_t) - row_dot)).astype(BF16)
        outs = (
            dot(k_t, d_scores) * SCALING,
            dot(q_t, d_scores, NT) * SCALING,
            dot(o_t, low_ref[h], NT),
        )
        for t in range(3):
            lo = 96 * t + HD * h
            for d in range(4):
                a_back[d, lo : lo + HD, :] = outs[t][:, ROWS * d : ROWS * d + ROWS].astype(BF16)

    near_back(0)
    arrived(pa_in)
    piece = pa_own[x, m]
    for r in range(7):
        piece += pa_recv[r].astype(F32)
    za[z] = piece.astype(BF16)
    za_in = [
        send(za.at[z], za.at[z], za_ss.at[r - 1], za_rs.at[r - 1], z_peer(r))
        for r in (4, 3, 5, 2, 6, 1, 7)
    ]
    near_back(1)
    a_ret[pos] = a_back[pos]
    ar_in = [
        send(
            a_back.at[(pos + r) % 4], a_ret.at[pos],
            ar_ss.at[r - 1], ar_rs.at[r - 1], (first + (pos + r) % 4, x),
        )
        for r in range(1, 4)
    ]

    arrived(dkv_in)
    dkv = dkv_recv[0].astype(F32)
    for r in range(1, 8):
        dkv += dkv_recv[r].astype(F32)
    b_back[...] = jnp.concatenate([tops(far_dq), tops(dkv)], axis=1).astype(BF16)
    b_ret[z] = b_back[z]
    br_in = [
        send(b_back.at[(z + r) % 8], b_ret.at[z], br_ss.at[r - 1], br_rs.at[r - 1], z_peer(r))
        for r in range(1, 8)
    ]

    scale = 32768.0 ** -0.5
    mine = z % 2 == core

    def total(ref):
        piece = ref[0].astype(F32)
        for r in range(1, 8):
            piece += ref[r].astype(F32)
        return (piece * scale).astype(BF16)

    def g1b_copy(r):
        slot = g1.at[1, z // 2]
        return pltpu.make_async_remote_copy(
            src_ref=slot, dst_ref=slot, send_sem=g1b_ss.at[r - 1], recv_sem=g1b_rs.at[r - 1],
            device_id=z_peer(r), device_id_type=MESH,
        )

    arrived(tb_in)
    tb_total = total(tb)

    @pl.when(mine)
    def _():
        g1[1, z // 2] = tb_total
        for r in (4, 3, 5, 2, 6, 1, 7):
            g1b_copy(r).start()

    arrived(za_in)
    g1[0, x] = total(za)
    g1a_in = [
        send(g1.at[0, x], g1.at[0, x], g1a_ss.at[r - 1], g1a_rs.at[r - 1], x_peer(r))
        for r in (2, 1, 3)
    ]

    arrived(ar_in)
    for t, ref in ((0, dq_ref), (1, dk_ref), (2, dv_ref)):
        ref[:, :HALF] = turn(
            jnp.concatenate([a_ret[s, 96 * t : 96 * t + 96, :] for s in range(4)], axis=0)
        )

    own = (y, x)

    def g2_sends(i, peer):
        copies = [
            send(g1.at[i], g2.at[i, own[i]], g2_ss.at[i, r - 1], g2_rs.at[i, r - 1], peer(r))
            for r in (2, 1, 3)
        ]
        send(g1.at[i], g3.at[i, own[i]], g3_ss.at[i, 0], g3_rs.at[i, 0], partner)
        g2[i, own[i]] = g1[i]
        return copies

    arrived(g1a_in)
    g2a_in = g2_sends(0, y_peer)

    @pl.when(mine)
    def _():
        for r in (2, 4, 6):
            g1b_copy(r).wait_recv()

    @pl.when(jnp.logical_not(mine))
    def _():
        for r in (1, 3, 5, 7):
            g1b_copy(r).wait_recv()

    g2b_in = g2_sends(1, x_peer)

    arrived(br_in)
    rows = b_ret[...].astype(F32)
    back_q = rows[:, :8, :].reshape(64, ROWS).astype(BF16)
    back_kv = rows[:, 8:, :].reshape(64, ROWS).astype(BF16)
    r64 = iota((ROWS, 64), 1)
    place = one_hot(iota((ROWS, 64), 0) == 16 * (r64 & 7) + (r64 >> 3))

    def spread(block, fold):
        rows = jnp.where(own_lanes, dot(block, fold, NT), 0.0).astype(BF16)
        return dot(place, rows).astype(BF16)

    dq_ref[:, far] = spread(back_q, fold0)
    dk_ref[:, far] = spread(back_kv, fold0)
    dv_ref[:, far] = spread(back_kv, fold1)

    for j, r in enumerate((2, 1, 3)):
        for i, copies in ((0, g2a_in), (1, g2b_in)):
            arrived([copies[j]])
            slot = (own[i] + 4 - r) % 4
            send(g2.at[i, slot], g3.at[i, slot], g3_ss.at[i, r], g3_rs.at[i, r], partner)

    def put(ref, c):
        for s in range(4):
            at = pl.multiple_of(96 * ((s % 2) * 2 + c), 96)
            dw_ref[pl.ds(at, 96), HALF * (s // 2) : HALF * (s // 2) + HALF] = (
                ref[0, s].astype(F32).reshape(96, HALF)
            )
            for k in range(4):
                at = pl.multiple_of(HALF + HD * (2 * k + c) + 24 * (s // 2), 8)
                dw_ref[pl.ds(at, 24), HALF * (s % 2) : HALF * (s % 2) + HALF] = (
                    ref[1, s, k].astype(F32)
                )

    put(g2, core)
    for i in range(2):
        for r in range(4):
            pltpu.make_async_copy(g3.at[i, 0], g3.at[i, 0], g3_rs.at[i, r]).wait()
    put(g3, 1 - core)

    for copy in started:
        copy.wait_send()

    @pl.when(mine)
    def _():
        for r in range(1, 8):
            g1b_copy(r).wait_send()


def pass_on(*refs):
    ins, outs, held, in_sem, out_sem = refs[:4], refs[4:8], refs[8:12], refs[12], refs[13]
    chunks = [(i, slice(None)) for i in range(3)]
    chunks += [(3, pl.ds(192 * j, 192)) for j in range(4)]
    arriving = []
    for n, (i, at) in enumerate(chunks):
        arriving.append(
            pltpu.make_async_copy(ins[i].at[at], held[i].at[at], in_sem.at[n])
        )
        arriving[-1].start()
    leaving = []
    for n, (i, at) in enumerate(chunks):
        arriving[n].wait()
        leaving.append(
            pltpu.make_async_copy(held[i].at[at], outs[i].at[at], out_sem.at[n])
        )
        leaving[-1].start()
    for copy in leaving:
        copy.wait()


def per_device(queries, keys, values, grad_out, w_out, kept_tiles):
    vmem = pl.BlockSpec(memory_space=pltpu.VMEM)
    anywhere = pl.BlockSpec(memory_space=pl.ANY)
    dma = pltpu.SemaphoreType.DMA
    block = jax.ShapeDtypeStruct((ROWS, WIDTH), BF16)
    out_shape = (block, block, block, jax.ShapeDtypeStruct((WIDTH, WIDTH), F32))
    outs = pl.pallas_call(
        kernel,
        out_shape=out_shape,
        in_specs=[pl.BlockSpec(memory_space=pltpu.SMEM)] + [vmem] * 5,
        out_specs=(vmem,) * 4,
        scratch_shapes=[
            pltpu.VMEM((4, HALF, ROWS), BF16),
            pltpu.VMEM((4, HALF, ROWS), BF16),
            pltpu.VMEM((4, 288, ROWS), BF16),
            pltpu.VMEM((4, 288, ROWS), BF16),
            pltpu.VMEM((4, ROWS, WIDTH), BF16),
            pltpu.VMEM((2, SEG, SEG), F32),
            pltpu.VMEM((2, SEG, SEG), BF16),
            pltpu.VMEM((8, 16, SEG), BF16),
            pltpu.VMEM((8, 16, SEG), BF16),
            pltpu.VMEM((8, 64, ROWS), BF16),
            pltpu.VMEM((8, 64, ROWS), BF16),
            pltpu.VMEM((8, 64, ROWS), BF16),
            pltpu.VMEM((8, 16, ROWS), BF16),
            pltpu.VMEM((8, 16, ROWS), BF16),
            pltpu.VMEM((4, 2) + PART, F32),
            pltpu.VMEM((4, 2) + PART, BF16),
            pltpu.VMEM((7,) + PART, BF16),
            pltpu.VMEM((4,) + PART, F32),
            pltpu.VMEM((4,) + PART, BF16),
            pltpu.VMEM((3,) + PART, BF16),
            pltpu.VMEM((8,) + PART, BF16),
            pltpu.VMEM((8,) + PART, BF16),
            pltpu.VMEM((2, 4) + PART, BF16),
            pltpu.VMEM((2, 4, 4) + PART, BF16),
            pltpu.VMEM((2, 4, 4) + PART, BF16),
            dma((3,)), dma((3,)), dma((3,)), dma((3,)), dma((3,)), dma((3,)),
            dma((7,)), dma((7,)), dma((7,)), dma((7,)), dma((7,)), dma((7,)),
            dma((7,)), dma((7,)), dma((7,)), dma((7,)), dma((3,)), dma((3,)),
            dma((7,)), dma((7,)), dma((7,)), dma((7,)),
            dma((3,)), dma((3,)), dma((7,)), dma((7,)), dma((2, 3)), dma((2, 3)),
            dma((2, 4)), dma((2, 4)),
        ],
        compiler_params=pltpu.CompilerParams(
            collective_id=0, has_side_effects=True, vmem_limit_bytes=56 * 1024 * 1024
        ),
        name="grouped_attention_grads",
    )(kept_tiles, queries[0], keys[0], values[0], grad_out[0], w_out)
    outs = pl.pallas_call(
        pass_on,
        out_shape=out_shape,
        in_specs=[anywhere] * 4,
        out_specs=(anywhere,) * 4,
        scratch_shapes=[pltpu.VMEM(s.shape, s.dtype) for s in out_shape]
        + [dma((7,)), dma((7,))],
        name="pass_on",
    )(*outs)
    return (outs[0][None], outs[1][None], outs[2][None], outs[3])


def solution(mesh):
    rows = P("slide", "seq", None)
    return jax.shard_map(
        per_device,
        mesh=mesh,
        in_specs=(rows, rows, rows, rows, P(), P("slide")),
        out_specs=(rows, rows, rows, P()),
        check_vma=False,
    )
```

```python
import jax
import jax.numpy as jnp
from jax import lax
from jax.experimental import pallas as pl
from jax.experimental.pallas import tpu as pltpu
from jax.sharding import PartitionSpec as P

ROWS = 128
WIDTH = 768
HALF = 384
HD = 48
SEG = 512
PART = (24, HALF)
F32 = jnp.float32
BF16 = jnp.bfloat16
MESH = pl.DeviceIdType.MESH
NN = (((1,), (0,)), ((), ()))
NT = (((1,), (1,)), ((), ()))
SCALING = HD ** -0.5


def dot(a, b, dims=NN):
    return lax.dot_general(a, b, dims, preferred_element_type=F32)


def iota(shape, dim):
    return lax.broadcasted_iota(jnp.int32, shape, dim)


def one_hot(mask):
    return jnp.where(mask, 1.0, 0.0).astype(BF16)


def turn(a):
    return jnp.transpose(a.astype(F32)).astype(BF16)


def softmax(scores, key_ok):
    scores = jnp.where(key_ok, scores * SCALING, -1e30)
    grown = jnp.exp(scores - jnp.max(scores, axis=0, keepdims=True))
    return grown * (1.0 / jnp.sum(grown, axis=0, keepdims=True))


def kernel(
    kept_ref, q_in, k_in, v_in, g_in, w_in,
    dq_ref, dk_ref, dv_ref, dw_ref,
    q_ref, k_ref, v_ref, w_ref, load_sem,
    a_send, a_recv, a_back, a_ret, g_all, probs_ref, low_ref,
    b_send, b_recv, kv_all, dkv_send, dkv_recv, b_back, b_ret,
    pa_own, pa_send, pa_recv, pb_own, pb_send, pb_recv, za, tb, g1, g2, g3,
    a_ss, a_rs, ar_ss, ar_rs, gr_ss, gr_rs, b_ss, b_rs, kv_ss, kv_rs, dkv_ss, dkv_rs,
    br_ss, br_rs, pa_ss, pa_rs, pb_ss, pb_rs, za_ss, za_rs, tb_ss, tb_rs,
    g1a_ss, g1a_rs, g1b_ss, g1b_rs, g2_ss, g2_rs, g3_ss, g3_rs,
):
    seq = lax.axis_index("seq")
    x = lax.axis_index("slide")
    core = seq % 2
    y = (seq // 2) % 4
    z = seq // 8
    pos = seq % 4
    tee = seq % 8
    first = seq - pos
    m = y // 2

    def x_peer(r):
        return (seq, (x + r) % 4)

    def y_peer(r):
        return ((z * 4 + (y + r) % 4) * 2 + core, x)

    def z_peer(r):
        return (((z + r) % 8) * 8 + tee, x)

    def plane_peer(r):
        return (z * 8 + (tee + r) % 8, x)

    def xm_peer(rx, rm):
        return ((z * 4 + (y + 2 * rm) % 4) * 2 + core, (x + rx) % 4)

    partner = (seq + 1 - 2 * core, x)
    across = (first + (pos + 2) % 4, x)

    started = []

    def send(src, dst, ss, rs, device):
        copy = pltpu.make_async_remote_copy(
            src_ref=src, dst_ref=dst, send_sem=ss, recv_sem=rs,
            device_id=device, device_id_type=MESH,
        )
        copy.start()
        started.append(copy)
        return copy

    def arrived(copies):
        for copy in copies:
            copy.wait_recv()

    barrier = pltpu.get_barrier_semaphore()

    def greet(device):
        pl.semaphore_signal(barrier, inc=1, device_id=device, device_id_type=MESH)

    for r in range(1, 8):
        greet(z_peer(r))
    for r in range(1, 8):
        greet(plane_peer(r))
    for rx in range(1, 4):
        for rm in range(2):
            greet(xm_peer(rx, rm))

    loads = [
        pltpu.make_async_copy(src, dst, load_sem.at[n])
        for n, (src, dst) in enumerate(
            ((k_in, k_ref), (q_in, q_ref), (v_in, v_ref), (g_in, g_all.at[pos]), (w_in, w_ref))
        )
    ]
    for copy in loads:
        copy.start()
    kept = kept_ref[0]
    far = pl.ds(HALF, HALF)
    for copy in loads[:4]:
        copy.wait()
    r64 = iota((64, ROWS), 0)
    pick = one_hot(iota((64, ROWS), 1) == 16 * (r64 & 7) + (r64 >> 3))
    l_in = iota((64, HALF), 1) - HD * (iota((64, HALF), 0) >> 3)
    own_lanes = (l_in >= 0) & (l_in < HD)
    feat = iota((HALF, ROWS), 0)
    feat = feat - HD * ((feat * 683) >> 15)
    lane = iota((HALF, ROWS), 1)
    fold0 = one_hot(lane == feat)
    fold1 = one_hot(lane == feat + HD)

    def dilated(block):
        rows = dot(pick, block)
        return jnp.where(own_lanes, rows, 0.0).astype(BF16)

    def tops(block):
        return block.reshape(8, 8, block.shape[-1])

    far_k = dot(dilated(k_ref[:, far]), fold0)
    far_qv = dot(dilated(q_ref[:, far]), fold0) + dot(dilated(v_ref[:, far]), fold1)
    far_g = dot(pick, g_all[pos])
    b_send[:, :, :ROWS] = jnp.concatenate([tops(far_k), tops(far_qv)], axis=1).astype(BF16)
    b_send[:, :, ROWS:] = jnp.concatenate(
        [tops(far_g[:, :HALF]), tops(far_g[:, HALF:])], axis=1
    ).astype(BF16)
    b_recv[z] = b_send[z]

    pl.semaphore_wait(barrier, 20)

    b_in = [
        send(b_send.at[(z + r) % 8], b_recv.at[z], b_ss.at[r - 1], b_rs.at[r - 1], z_peer(r))
        for r in (4, 3, 5, 2, 6, 1, 7)
    ]
    g_across = send(g_all.at[pos], g_all.at[pos], gr_ss.at[0], gr_rs.at[0], across)
    g_near = send(g_all.at[pos], g_all.at[pos], gr_ss.at[1], gr_rs.at[1], partner)

    near = (turn(q_ref[:, :HALF]), turn(k_ref[:, :HALF]), turn(v_ref[:, :HALF]))
    for d in range(4):
        for t in range(3):
            a_send[d, 96 * t : 96 * t + 96, :] = near[t][96 * d : 96 * d + 96]
    a_recv[pos] = a_send[pos]

    a_in = [
        send(
            a_send.at[(pos + r) % 4], a_recv.at[pos],
            a_ss.at[r - 1], a_rs.at[r - 1], (first + (pos + r) % 4, x),
        )
        for r in range(1, 4)
    ]
    arrived(b_in)
    rows = b_recv[:, :, :ROWS].astype(F32)
    k_rows = rows[:, :8, :].reshape(64, ROWS)
    qv = rows[:, 8:, :].reshape(64, ROWS)
    lane64 = iota((64, ROWS), 1)
    left = lane64 < HD
    right = (lane64 >= HD) & (lane64 < 2 * HD)
    kv_all[tee] = jnp.where(left, k_rows, jnp.where(right, qv, 0.0)).astype(BF16)
    kv_in = [
        send(kv_all.at[tee], kv_all.at[tee], kv_ss.at[r - 1], kv_rs.at[r - 1], plane_peer(r))
        for r in range(1, 8)
    ]
    q_rows = jnp.where(left, qv, 0.0).astype(BF16)
    q_cols = turn(q_rows)

    loads[4].wait()

    arrived(a_in)
    at = first * ROWS
    key_ok = at + iota((SEG, 1), 0) < kept
    row_ok = jnp.where(at + iota((1, SEG), 1) < kept, 1.0, 0.0)

    def head_rows(t, h):
        lo = 96 * t + HD * h
        return jnp.concatenate([a_recv[s, lo : lo + HD, :] for s in range(4)], axis=1)

    attn_near = []
    for h in range(2):
        probs = softmax(dot(turn(head_rows(1, h)), head_rows(0, h)), key_ok)
        low = probs.astype(BF16)
        probs_ref[h] = probs
        low_ref[h] = low
        attn_near.append((dot(head_rows(2, h), low) * row_ok).astype(BF16))

    arrived([g_across])
    g_fwd = send(
        g_all.at[(pos + 2) % 4], g_all.at[(pos + 2) % 4], gr_ss.at[2], gr_rs.at[2], partner
    )

    arrived(kv_in)
    kv = kv_all[...].reshape(SEG, ROWS)
    kv_cols = turn(kv)
    r512 = iota((SEG, 1), 0)
    far_key_ok = (
        (((r512 >> 3) & 7) * 8 + (r512 >> 6)) * ROWS + 16 * (r512 & 7) + z < kept
    )
    c64 = iota((1, 64), 1)
    far_row_ok = jnp.where(((c64 >> 3) * 8 + tee) * ROWS + 16 * (c64 & 7) + z < kept, 1.0, 0.0)
    far_probs = softmax(dot(kv, q_cols), far_key_ok)
    far_low = far_probs.astype(BF16)
    attn_far = (dot(kv_cols, far_low) * far_row_ok).astype(BF16)
    rows = b_recv[:, :, ROWS:].astype(F32)
    far_g = [rows[:, 8 * i : 8 * i + 8, :].reshape(64, HALF).astype(BF16) for i in range(2)]
    for i in range(2):
        block = dot(attn_far[HD : 2 * HD], far_g[i])
        for half in range(2):
            piece = block[24 * half : 24 * half + 24]
            pb_own[2 * half + i] = piece
            pb_send[2 * half + i] = piece.astype(BF16)
    pb_in = [
        send(pb_send.at[(x + r) % 4], pb_recv.at[r - 1], pb_ss.at[r - 1], pb_rs.at[r - 1], x_peer(r))
        for r in range(1, 4)
    ]

    arrived([g_near, g_fwd])
    attn = jnp.concatenate(attn_near, axis=0)
    block = dot(attn, g_all[...].reshape(SEG, WIDTH))
    for i in range(4):
        for j in range(2):
            piece = block[24 * i : 24 * i + 24, HALF * j : HALF * j + HALF]
            pa_own[i, j] = piece
            pa_send[i, j] = piece.astype(BF16)
    pa_in = [
        send(
            pa_send.at[(x + rx) % 4, (m + rm) % 2], pa_recv.at[2 * rx + rm - 1],
            pa_ss.at[2 * rx + rm - 1], pa_rs.at[2 * rx + rm - 1], xm_peer(rx, rm),
        )
        for rx, rm in ((2, 1), (1, 1), (3, 1), (2, 0), (1, 0), (3, 0), (0, 1))
    ]

    w_at = pl.multiple_of(HALF + HD * z, 16)
    d_attn = sum(
        dot(w_ref[pl.ds(w_at, HD), HALF * i : HALF * i + HALF], far_g[i], NT) for i in range(2)
    )
    pad = jnp.zeros((HD, 64), F32)
    o_cols = jnp.concatenate([pad, d_attn * far_row_ok, pad[: ROWS - 2 * HD]], axis=0).astype(BF16)
    o_rows = turn(o_cols)
    row_dot = jnp.sum(o_cols.astype(F32) * attn_far.astype(F32), axis=0, keepdims=True)
    far_ds = (far_probs * (dot(kv, o_cols) - row_dot)).astype(BF16)
    far_dq = jnp.transpose(dot(kv_cols, far_ds) * SCALING)
    dkv = dot(far_ds, q_rows) * SCALING + dot(far_low, o_rows)
    dkv = dkv.reshape(8, 64, ROWS)
    dkv_send[...] = dkv.astype(BF16)
    dkv_recv[tee] = dkv_send[tee]
    dkv_in = [
        send(
            dkv_send.at[(tee + r) % 8], dkv_recv.at[tee],
            dkv_ss.at[r - 1], dkv_rs.at[r - 1], plane_peer(r),
        )
        for r in range(1, 8)
    ]

    arrived(pb_in)
    piece = pb_own[x]
    for r in range(3):
        piece += pb_recv[r].astype(F32)
    tb[tee] = piece.astype(BF16)
    tb_in = [
        send(tb.at[tee], tb.at[tee], tb_ss.at[r - 1], tb_rs.at[r - 1], plane_peer(r))
        for r in range(1, 8)
    ]

    w_at = pl.multiple_of(96 * pos, 96)
    d_attn = (dot(w_ref[pl.ds(w_at, 96), :], g_all[...].reshape(SEG, WIDTH), NT) * row_ok).astype(BF16)

    def near_back(h):
        q_t, k_t, v_t = (head_rows(t, h) for t in range(3))
        o_t = d_attn[HD * h : HD * h + HD]
        row_dot = jnp.sum(o_t.astype(F32) * attn_near[h].astype(F32), axis=0, keepdims=True)
        d_scores = (probs_ref[h] * (dot(turn(v_t), o_t) - row_dot)).astype(BF16)
        outs = (
            dot(k_t, d_scores) * SCALING,
            dot(q_t, d_scores, NT) * SCALING,
            dot(o_t, low_ref[h], NT),
        )
        for t in range(3):
            lo = 96 * t + HD * h
            for d in range(4):
                a_back[d, lo : lo + HD, :] = outs[t][:, ROWS * d : ROWS * d + ROWS].astype(BF16)

    near_back(0)
    arrived(pa_in)
    piece = pa_own[x, m]
    for r in range(7):
        piece += pa_recv[r].astype(F32)
    za[z] = piece.astype(BF16)
    za_in = [
        send(za.at[z], za.at[z], za_ss.at[r - 1], za_rs.at[r - 1], z_peer(r))
        for r in (4, 3, 5, 2, 6, 1, 7)
    ]
    near_back(1)
    a_ret[pos] = a_back[pos]
    ar_in = [
        send(
            a_back.at[(pos + r) % 4], a_ret.at[pos],
            ar_ss.at[r - 1], ar_rs.at[r - 1], (first + (pos + r) % 4, x),
        )
        for r in range(1, 4)
    ]

    arrived(dkv_in)
    dkv = dkv_recv[0].astype(F32)
    for r in range(1, 8):
        dkv += dkv_recv[r].astype(F32)
    b_back[...] = jnp.concatenate([tops(far_dq), tops(dkv)], axis=1).astype(BF16)
    b_ret[z] = b_back[z]
    br_in = [
        send(b_back.at[(z + r) % 8], b_ret.at[z], br_ss.at[r - 1], br_rs.at[r - 1], z_peer(r))
        for r in range(1, 8)
    ]

    scale = 32768.0 ** -0.5
    mine = z % 2 == core

    def total(ref):
        piece = ref[0].astype(F32)
        for r in range(1, 8):
            piece += ref[r].astype(F32)
        return (piece * scale).astype(BF16)

    def g1b_copy(r):
        slot = g1.at[1, z // 2]
        return pltpu.make_async_remote_copy(
            src_ref=slot, dst_ref=slot, send_sem=g1b_ss.at[r - 1], recv_sem=g1b_rs.at[r - 1],
            device_id=z_peer(r), device_id_type=MESH,
        )

    arrived(tb_in)
    tb_total = total(tb)

    @pl.when(mine)
    def _():
        g1[1, z // 2] = tb_total
        for r in (4, 3, 5, 2, 6, 1, 7):
            g1b_copy(r).start()

    arrived(za_in)
    g1[0, x] = total(za)
    g1a_in = [
        send(g1.at[0, x], g1.at[0, x], g1a_ss.at[r - 1], g1a_rs.at[r - 1], x_peer(r))
        for r in (2, 1, 3)
    ]

    arrived(ar_in)
    for t, ref in ((0, dq_ref), (1, dk_ref), (2, dv_ref)):
        ref[:, :HALF] = turn(
            jnp.concatenate([a_ret[s, 96 * t : 96 * t + 96, :] for s in range(4)], axis=0)
        )

    own = (y, x)

    def g2_sends(i, peer):
        copies = [
            send(g1.at[i], g2.at[i, own[i]], g2_ss.at[i, r - 1], g2_rs.at[i, r - 1], peer(r))
            for r in (2, 1, 3)
        ]
        send(g1.at[i], g3.at[i, own[i]], g3_ss.at[i, 0], g3_rs.at[i, 0], partner)
        g2[i, own[i]] = g1[i]
        return copies

    arrived(g1a_in)
    g2a_in = g2_sends(0, y_peer)

    @pl.when(mine)
    def _():
        for r in (2, 4, 6):
            g1b_copy(r).wait_recv()

    @pl.when(jnp.logical_not(mine))
    def _():
        for r in (1, 3, 5, 7):
            g1b_copy(r).wait_recv()

    g2b_in = g2_sends(1, x_peer)

    arrived(br_in)
    rows = b_ret[...].astype(F32)
    back_q = rows[:, :8, :].reshape(64, ROWS).astype(BF16)
    back_kv = rows[:, 8:, :].reshape(64, ROWS).astype(BF16)
    r64 = iota((ROWS, 64), 1)
    place = one_hot(iota((ROWS, 64), 0) == 16 * (r64 & 7) + (r64 >> 3))

    def spread(block, fold):
        rows = jnp.where(own_lanes, dot(block, fold, NT), 0.0).astype(BF16)
        return dot(place, rows).astype(BF16)

    dq_ref[:, far] = spread(back_q, fold0)
    dk_ref[:, far] = spread(back_kv, fold0)
    dv_ref[:, far] = spread(back_kv, fold1)

    for j, r in enumerate((2, 1, 3)):
        for i, copies in ((0, g2a_in), (1, g2b_in)):
            arrived([copies[j]])
            slot = (own[i] + 4 - r) % 4
            send(g2.at[i, slot], g3.at[i, slot], g3_ss.at[i, r], g3_rs.at[i, r], partner)

    def put(ref, c):
        for s in range(4):
            at = pl.multiple_of(96 * ((s % 2) * 2 + c), 96)
            dw_ref[pl.ds(at, 96), HALF * (s // 2) : HALF * (s // 2) + HALF] = (
                ref[0, s].astype(F32).reshape(96, HALF)
            )
            for k in range(4):
                at = pl.multiple_of(HALF + HD * (2 * k + c) + 24 * (s // 2), 8)
                dw_ref[pl.ds(at, 24), HALF * (s % 2) : HALF * (s % 2) + HALF] = (
                    ref[1, s, k].astype(F32)
                )

    put(g2, core)
    for i in range(2):
        for r in range(4):
            pltpu.make_async_copy(g3.at[i, 0], g3.at[i, 0], g3_rs.at[i, r]).wait()
    put(g3, 1 - core)

    for copy in started:
        copy.wait_send()

    @pl.when(mine)
    def _():
        for r in range(1, 8):
            g1b_copy(r).wait_send()


def pass_on(*refs):
    ins, outs, sem = refs[:4], refs[4:8], refs[8]
    copies = [
        pltpu.make_async_copy(ins[i].at[at], outs[i].at[at], sem.at[n])
        for n, (i, at) in enumerate(
            [(3, pl.ds(192 * j, 192)) for j in range(4)] + [(i, slice(None)) for i in range(3)]
        )
    ]
    for copy in copies:
        copy.start()
    for copy in copies:
        copy.wait()


def per_device(queries, keys, values, grad_out, w_out, kept_tiles):
    vmem = pl.BlockSpec(memory_space=pltpu.VMEM)
    anywhere = pl.BlockSpec(memory_space=pl.ANY)
    dma = pltpu.SemaphoreType.DMA
    block = jax.ShapeDtypeStruct((ROWS, WIDTH), BF16)
    out_shape = (block, block, block, jax.ShapeDtypeStruct((WIDTH, WIDTH), F32))
    outs = pl.pallas_call(
        kernel,
        out_shape=tuple(pltpu.VMEM(s.shape, s.dtype) for s in out_shape),
        in_specs=[pl.BlockSpec(memory_space=pltpu.SMEM)] + [anywhere] * 5,
        out_specs=(vmem,) * 4,
        scratch_shapes=[
            pltpu.VMEM((ROWS, WIDTH), BF16),
            pltpu.VMEM((ROWS, WIDTH), BF16),
            pltpu.VMEM((ROWS, WIDTH), BF16),
            pltpu.VMEM((WIDTH, WIDTH), BF16),
            dma((5,)),
            pltpu.VMEM((4, 288, ROWS), BF16),
            pltpu.VMEM((4, 288, ROWS), BF16),
            pltpu.VMEM((4, 288, ROWS), BF16),
            pltpu.VMEM((4, 288, ROWS), BF16),
            pltpu.VMEM((4, ROWS, WIDTH), BF16),
            pltpu.VMEM((2, SEG, SEG), F32),
            pltpu.VMEM((2, SEG, SEG), BF16),
            pltpu.VMEM((8, 16, SEG), BF16),
            pltpu.VMEM((8, 16, SEG), BF16),
            pltpu.VMEM((8, 64, ROWS), BF16),
            pltpu.VMEM((8, 64, ROWS), BF16),
            pltpu.VMEM((8, 64, ROWS), BF16),
            pltpu.VMEM((8, 16, ROWS), BF16),
            pltpu.VMEM((8, 16, ROWS), BF16),
            pltpu.VMEM((4, 2) + PART, F32),
            pltpu.VMEM((4, 2) + PART, BF16),
            pltpu.VMEM((7,) + PART, BF16),
            pltpu.VMEM((4,) + PART, F32),
            pltpu.VMEM((4,) + PART, BF16),
            pltpu.VMEM((3,) + PART, BF16),
            pltpu.VMEM((8,) + PART, BF16),
            pltpu.VMEM((8,) + PART, BF16),
            pltpu.VMEM((2, 4) + PART, BF16),
            pltpu.VMEM((2, 4, 4) + PART, BF16),
            pltpu.VMEM((2, 4, 4) + PART, BF16),
            dma((3,)), dma((3,)), dma((3,)), dma((3,)), dma((3,)), dma((3,)),
            dma((7,)), dma((7,)), dma((7,)), dma((7,)), dma((7,)), dma((7,)),
            dma((7,)), dma((7,)), dma((7,)), dma((7,)), dma((3,)), dma((3,)),
            dma((7,)), dma((7,)), dma((7,)), dma((7,)),
            dma((3,)), dma((3,)), dma((7,)), dma((7,)), dma((2, 3)), dma((2, 3)),
            dma((2, 4)), dma((2, 4)),
        ],
        compiler_params=pltpu.CompilerParams(
            collective_id=0, has_side_effects=True, vmem_limit_bytes=56 * 1024 * 1024
        ),
        name="grouped_attention_grads",
    )(kept_tiles, queries[0], keys[0], values[0], grad_out[0], w_out)
    outs = pl.pallas_call(
        pass_on,
        out_shape=out_shape,
        in_specs=[vmem] * 4,
        out_specs=(anywhere,) * 4,
        scratch_shapes=[dma((7,))],
        name="pass_on",
    )(*[pltpu.with_memory_space_constraint(out, pltpu.VMEM) for out in outs])
    return (outs[0][None], outs[1][None], outs[2][None], outs[3])


def solution(mesh):
    rows = P("slide", "seq", None)
    return jax.shard_map(
        per_device,
        mesh=mesh,
        in_specs=(rows, rows, rows, rows, P(), P("slide")),
        out_specs=(rows, rows, rows, P()),
        check_vma=False,
    )
```
